32 devices in a mesh: groups: 2 (over y), row: 4 (over z), col: 4 (over x, core).
Axes of the slice: x: 2, y: 2, z: 4, core: 2. Of those that a mesh axis runs over, the one named last changes fastest.
Arguments:
- pair: bfloat16 [512, 256, 128], P(('groups', 'row'), 'col'), parts along dimension 0, may hold values from -300 to 300
- single: bfloat16 [512, 384], P(('groups', 'row')), parts along dimension 0, may hold values from -6 to 6
- token_mask: int32 [512], P(('groups', 'col')), parts along dimension 0, may hold values from 0 to 1, as said below
- pair_gain: float32 [128], replicated, may hold values from 0.25 to 1.75
- transition_in: bfloat16 [128, 1024], replicated, may hold values from -0.5 to 0.5
- transition_out: bfloat16 [512, 128], replicated, may hold values from -0.25 to 0.25
- bias_weight: float32 [128, 16], replicated, may hold values from -0.9 to 0.9
- bin_weight: float32 [128, 64], replicated, may hold values from -0.5 to 0.5
- single_gain: float32 [384], replicated, may hold values from 0.25 to 1.75
- attention_in: bfloat16 [384, 1536], replicated, may hold values from -0.3125 to 0.3125
- attention_out: bfloat16 [384, 384], replicated, may hold values from -0.8984375 to 0.8984375
Outputs:
- distogram: float32 [512, 256, 64], P(('groups', 'row'), 'col'), parts along dimension 0
- single_update: bfloat16 [512, 384], P(('groups', 'row')), parts along dimension 0
The draws below stay inside these ranges and needn't reach their ends.
There are 2 independent parts, one for each index of `groups`. The reference program is written for one: setup_inputs(seed, part) draws one part's arguments, and reference() takes and returns one part's arrays. A program takes and returns all parts, laid end to end along the dimension named above; an argument that names none is the same for every part. Nothing has to cross between parts.
Inputs may be any that keep to these rules, and one draw needn't show every extreme that they name: `token_mask`: 1 on a prefix of at least 128 tokens, 0 after it; at least the last token is 0.
All inputs are finite; a program needn't handle non-finite values.
Results may differ from the reference program's by a relative error of at most 0.014.
Values may be sent and summed in bfloat16 or wider, within the bound.
A program may use at most 64 MiB of HBM per device.

```python
import math
import jax
import jax.numpy as jnp
from jax import lax

CP = 128
TRANS_HIDDEN = 512
HEADS = 16
HEAD_DIM = 24
BINS = 64
TILE = 64
CS = 384
TOKENS = 256


def draw_pair(key, part):
    shape = (TOKENS, TOKENS, CP)
    values = jnp.clip(jax.random.normal(key, shape, jnp.float32), -6.0, 6.0)
    return values.astype(jnp.bfloat16)


def draw_token_mask(key, part):
    valid_count = jax.random.randint(key, (), TOKENS // 2, TOKENS)
    return (jnp.arange(TOKENS) < valid_count).astype(jnp.int32)


def steps_of(own_key, shape, pieces, low, largest):
    def one(dim, parts):
        steps = jax.random.uniform(jax.random.fold_in(jax.random.fold_in(own_key, 6), dim), (parts,), jnp.float32, low / len(pieces), largest / len(pieces))
        return jnp.repeat(jnp.exp(steps), shape[dim] // parts).reshape((-1,) + (1,) * (len(shape) - dim - 1))

    loudness = one(*pieces[0])
    for cut in pieces[1:]:
        loudness = loudness * one(*cut)
    return loudness


def normal_values(key, shape, width, most, pieces=(), held_as=jnp.bfloat16):
    result = width * jax.random.normal(key, shape, jnp.float32)
    if pieces:
        result = result * steps_of(key, shape, pieces, -0.22, 0.18)
    return jnp.clip(result, -most, most).astype(held_as)


def setup_inputs(seed: int = 0, part: int = 0) -> dict:
    key_of = jax.random.split(jax.random.key(seed), 12)
    part_splits = jax.random.split(jax.random.fold_in(key_of[11], part), 12)
    return {
        "pair": draw_pair(jax.random.fold_in(jax.random.fold_in(key_of[11], part), 71), part),
        "single": normal_values(part_splits[1], (TOKENS, CS), 1.0, 6.0, ((0, 4),)),
        "token_mask": draw_token_mask(jax.random.fold_in(jax.random.fold_in(key_of[11], part), 71), part),
        "pair_gain": jnp.clip(1.0 + 0.15 * jax.random.normal(key_of[3], (CP,), jnp.float32), 0.25, 1.75),
        "transition_in": normal_values(key_of[4], (CP, 2 * TRANS_HIDDEN), CP ** -0.5, 0.5),
        "transition_out": normal_values(key_of[5], (TRANS_HIDDEN, CP), TRANS_HIDDEN ** -0.5, 0.25),
        "bias_weight": normal_values(key_of[6], (CP, HEADS), 0.15, 0.9, (), jnp.float32),
        "bin_weight": normal_values(key_of[7], (CP, BINS), CP ** -0.5, 0.5, (), jnp.float32),
        "single_gain": jnp.clip(1.0 + 0.15 * jax.random.normal(key_of[8], (CS,), jnp.float32), 0.25, 1.75),
        "attention_in": normal_values(key_of[9], (CS, 4 * CS), CS ** -0.5, 0.3125),
        "attention_out": normal_values(key_of[10], (CS, CS), 0.15, 0.8984375),
    }


def layer_norm(values, gain):
    average = lax.optimization_barrier(jnp.mean(values, axis=-1, keepdims=True))
    centered = values - average
    variance = lax.optimization_barrier(jnp.mean(centered * centered, axis=-1, keepdims=True))
    return centered * lax.rsqrt(variance + 1e-05) * gain

def pair_block(block_rows, pair_gain, transition_in, transition_out, bias_weight, bin_weight):
    count = block_rows.shape[0] * block_rows.shape[1]
    flat = block_rows.reshape(count, block_rows.shape[2]).astype(jnp.float32)
    normed = layer_norm(flat, pair_gain).astype(jnp.bfloat16)
    both = jnp.dot(normed, transition_in, preferred_element_type=jnp.float32)
    gated = (jax.nn.silu(both[:, :TRANS_HIDDEN]) * both[:, TRANS_HIDDEN:]).astype(jnp.bfloat16)
    updated = flat + jnp.dot(gated, transition_out, preferred_element_type=jnp.float32)
    biases = jnp.dot(updated, bias_weight, precision=lax.Precision.HIGHEST)
    halves = jnp.dot(updated, bin_weight, precision=lax.Precision.HIGHEST)
    return (biases.reshape(block_rows.shape[0], block_rows.shape[1], HEADS), halves.reshape(block_rows.shape[0], block_rows.shape[1], BINS))

def reference(pair, single, token_mask, pair_gain, transition_in, transition_out, bias_weight, bin_weight, single_gain, attention_in, attention_out):

    def per_block(block_rows):
        return pair_block(block_rows, pair_gain, transition_in, transition_out, bias_weight, bin_weight)
    blocks = pair.reshape(TOKENS // TILE, TILE, TOKENS, CP)
    biases, halves = lax.map(per_block, blocks)
    biases = biases.reshape(TOKENS, TOKENS, HEADS)
    halves = halves.reshape(TOKENS, TOKENS, BINS)
    distogram = jax.nn.softmax(halves + halves.transpose(1, 0, 2), axis=-1)
    normed = layer_norm(single.astype(jnp.float32), single_gain).astype(jnp.bfloat16)
    projected = jnp.dot(normed, attention_in, preferred_element_type=jnp.float32)
    queries = projected[:, :CS].reshape(TOKENS, HEADS, HEAD_DIM)
    keys_proj = projected[:, CS:2 * CS].reshape(TOKENS, HEADS, HEAD_DIM)
    values_proj = projected[:, 2 * CS:3 * CS].reshape(TOKENS, HEADS, HEAD_DIM)
    gates = projected[:, 3 * CS:]
    scores = jnp.einsum('ihd,jhd->ihj', queries, keys_proj) / math.sqrt(HEAD_DIM) + biases.transpose(0, 2, 1)
    scores = jnp.where(token_mask[None, None, :] > 0, scores, -1000000000.0)
    highest = lax.optimization_barrier(jnp.max(scores, axis=-1, keepdims=True))
    weights = jnp.exp(scores - highest)
    totals = lax.optimization_barrier(jnp.sum(weights, axis=-1))
    summed = jnp.einsum('ihj,jhd->ihd', weights, values_proj)
    attended = (summed / totals[..., None]).reshape(TOKENS, CS)
    gated = (jax.nn.sigmoid(gates) * attended).astype(jnp.bfloat16)
    single_update = jnp.dot(gated, attention_out, preferred_element_type=jnp.float32).astype(jnp.bfloat16)
    return (distogram, single_update)
```

```python
import functools
import math

import jax
import jax.numpy as jnp
from jax import lax
from jax.experimental import pallas as pl
from jax.experimental.pallas import tpu as pltpu
from jax.sharding import PartitionSpec as P

MESH = pl.DeviceIdType.MESH
F32 = jnp.float32
BF16 = jnp.bfloat16
LAG = 3


def dot(a, b):
    return jnp.dot(a, b, preferred_element_type=F32)


def layer_norm(values, gain):
    average = jnp.mean(values, axis=-1, keepdims=True)
    centered = values - average
    variance = jnp.mean(centered * centered, axis=-1, keepdims=True)
    return centered * lax.rsqrt(variance + 1e-05) * gain


def split(value):
    high = value.astype(BF16)
    return high, (value - high.astype(F32)).astype(BF16)


def kernel(
    side, chunks, relayed,
    pair_hbm, single_hbm, *rest,
):
    far = rest[:8]
    result, gated_out = rest[8:10]
    pair, single, *near = rest[10:20]
    mask, pair_gain, transition_in, transition_out, bias_t, bin_t, single_gain, attention_in = near
    pair_sem, load_sem = rest[20:22]
    (
        own, packed, mirrored, relay, key_rows, parts, first, second, normed, inner,
        queries, gates, keys, vals, spread, gather,
        key_send, key_recv, send_sem, recv_sem, relay_recv, relay_send, part_send, part_recv,
    ) = rest[22:]
    g, r, c = (lax.axis_index(name) for name in ("groups", "row", "col"))
    off = r != c
    diagonal = r == c
    tile_rows, width = single.shape
    tile_cols = key_rows.shape[0]
    heads = bias_t.shape[0]
    bins = bin_t.shape[0]
    head_width = width // heads
    hidden = transition_out.shape[0]
    lanes = pair.shape[1]
    half = tile_rows * tile_cols // 2
    n = half // chunks
    block = n // tile_cols

    def part(q):
        return pl.ds(pl.multiple_of(q * n, n), n)

    def upper(q):
        return pl.ds(pl.multiple_of(half + q * n, n), n)

    def load(q, side_half):
        rows = upper(q) if side_half else part(q)
        return pltpu.make_async_copy(pair_hbm.at[rows], pair.at[rows], pair_sem.at[side_half, q])

    loads = [
        pltpu.make_async_copy(source, target, load_sem.at[index])
        for index, (source, target) in enumerate(zip((single_hbm, *far), (single, *near)))
    ]
    for index in (0, 5, 6, 4, 2, 3):
        loads[index].start()
    for q in range(chunks):
        load(q, 0).start()
        load(q, 1).start()
    for index in (1, 7, 8):
        loads[index].start()

    barrier = pltpu.get_barrier_semaphore()
    for step in range(1, side):
        pl.semaphore_signal(barrier, inc=1, device_id=(g, r, lax.rem(c + step, side)), device_id_type=MESH)
        pl.semaphore_signal(barrier, inc=1, device_id=(g, lax.rem(r + step, side), c), device_id_type=MESH)

    @pl.when(off)
    def _():
        pl.semaphore_signal(barrier, inc=1, device_id=(g, c, r), device_id_type=MESH)

    loads[5].wait()
    loads[6].wait()
    stacked = jnp.concatenate(
        [bin_t[...], bias_t[...], jnp.zeros((lanes - heads - bins, lanes), F32)], axis=0
    ).T
    high, low = split(stacked)
    loads[4].wait()
    second[hidden:, :lanes] = high
    second[hidden:, lanes:] = low
    joint = dot(transition_out[...], second[hidden:])
    high, low = split(joint[:, :lanes] + joint[:, lanes:])
    second[:hidden, :lanes] = high
    second[:hidden, lanes:] = low
    feature = lax.broadcasted_iota(jnp.int32, (width, lanes), 0)
    head = lax.broadcasted_iota(jnp.int32, (width, lanes), 1) - bins
    gather[...] = jnp.where(
        (feature >= head * head_width) & (feature < (head + 1) * head_width), 1.0, 0.0
    ).astype(BF16)
    feature = lax.broadcasted_iota(jnp.int32, (lanes, width), 1)
    head = lax.broadcasted_iota(jnp.int32, (lanes, width), 0) - bins
    spread[...] = jnp.where(
        (feature >= head * head_width) & (feature < (head + 1) * head_width), 1.0, 0.0
    ).astype(BF16)

    @pl.when(off)
    def _():
        pl.semaphore_wait(barrier, 2 * (side - 1) + 1)

    @pl.when(diagonal)
    def _():
        pl.semaphore_wait(barrier, 2 * (side - 1))

    key_copy = pltpu.make_async_remote_copy(
        src_ref=single, dst_ref=key_rows, send_sem=key_send, recv_sem=key_recv,
        device_id=(g, c, r), device_id_type=MESH,
    )

    loads[0].wait()

    def direct(u):
        return pltpu.make_async_remote_copy(
            src_ref=packed.at[part(u)], dst_ref=mirrored.at[part(u)],
            send_sem=send_sem.at[u], recv_sem=recv_sem.at[u],
            device_id=(g, c, r), device_id_type=MESH,
        )

    def to_relay(t):
        u = relayed[t]
        return pltpu.make_async_remote_copy(
            src_ref=packed.at[part(u)], dst_ref=relay.at[c, part(t)],
            send_sem=send_sem.at[u], recv_sem=relay_recv.at[c, t],
            device_id=(g, r, r), device_id_type=MESH,
        )

    def forward(k, t):
        return pltpu.make_async_remote_copy(
            src_ref=relay.at[k, part(t)], dst_ref=mirrored.at[part(relayed[t])],
            send_sem=relay_send.at[k, t], recv_sem=recv_sem.at[relayed[t]],
            device_id=(g, k, r), device_id_type=MESH,
        )

    def arrived(k, t):
        return pltpu.make_async_remote_copy(
            src_ref=relay.at[k, part(t)], dst_ref=relay.at[k, part(t)],
            send_sem=relay_send.at[k, t], recv_sem=relay_recv.at[k, t],
            device_id=(g, k, r), device_id_type=MESH,
        )

    def forward_all(t):
        for step in range(1, side):
            k = lax.rem(r + step, side)
            arrived(k, t).wait_recv()
            forward(k, t).start()

    @pl.when(off)
    def _():
        key_copy.start()

    @pl.when(diagonal)
    def _():
        key_rows[...] = single[...]

    loads[2].wait()
    loads[3].wait()
    first[:, :hidden] = transition_in[:, :hidden] * jnp.asarray(0.5, BF16)
    first[:, hidden:] = transition_in[:, hidden:]
    wide = min(256, hidden)

    def slot(q):
        return pl.ds(pl.multiple_of(lax.rem(q, 2) * 2 * n, 2 * n), 2 * n)

    def tokens(q):
        return jnp.concatenate([pair[part(q)], pair[upper(q)]], axis=0)

    def norm(q):
        normed[slot(q)] = layer_norm(tokens(q).astype(F32), pair_gain[...]).astype(BF16)

    def expand(q):
        some = normed[slot(q)]
        for start in range(0, hidden, wide):
            gate = dot(some, first[:, start : start + wide])
            up = dot(some, first[:, hidden + start : hidden + start + wide])
            inner[slot(q), start : start + wide] = ((gate + gate * jnp.tanh(gate)) * up).astype(BF16)

    def project(q):
        both = dot(jnp.concatenate([inner[slot(q)], tokens(q)], axis=1), second[...])
        product = both[:, :lanes] + both[:, lanes:]
        own[part(q)] = product[:n]
        own[upper(q)] = product[n:]
        lane = lax.broadcasted_iota(jnp.int32, (n, lanes), 1)
        logits = 0.25 * jnp.where(lane < bins, product[:n], pltpu.roll(product[n:], bins, 1))
        square = logits * logits
        packed[part(q)] = (square * square * logits).astype(BF16)

    def ready(q):
        load(q, 0).wait()
        load(q, 1).wait()

    def send(q):
        for u in range(chunks):
            if u in relayed:
                @pl.when(off & (q == u))
                def _(u=u):
                    to_relay(relayed.index(u)).start()

            else:
                @pl.when(off & (q == u))
                def _(u=u):
                    direct(u).start()

        @pl.when(diagonal)
        def _():
            mirrored[part(q)] = packed[part(q)]

        for t, u in enumerate(relayed):
            if u + LAG < chunks:
                @pl.when(diagonal & (q == u + LAG))
                def _(t=t):
                    forward_all(t)

    ready(0)
    norm(0)
    ready(1)
    norm(1)
    expand(0)

    def transition(q, carry):
        ready(q + 2)
        project(q)
        expand(q + 1)
        norm(q + 2)
        send(q)
        return carry

    lax.fori_loop(0, chunks - 2, transition, 0)
    project(chunks - 2)
    expand(chunks - 1)
    send(chunks - 2)
    project(chunks - 1)
    send(chunks - 1)

    @pl.when(diagonal)
    def _():
        for t, u in enumerate(relayed):
            if u + LAG >= chunks:
                forward_all(t)

    for index in (1, 7, 8):
        loads[index].wait()
    single_scale = single_gain[...].reshape(1, width)
    query_normed = layer_norm(single[...].astype(F32), single_scale).astype(BF16)
    queries[...] = dot(query_normed, attention_in[:, :width]) * (1.0 / math.sqrt(head_width))
    gates[...] = dot(query_normed, attention_in[:, 3 * width :])

    @pl.when(off)
    def _():
        key_copy.wait()

    key_normed = layer_norm(key_rows[...].astype(F32), single_scale).astype(BF16)
    keys[...] = dot(key_normed, attention_in[:, width : 2 * width])
    vals[...] = dot(key_normed, attention_in[:, 2 * width : 3 * width])
    group = 8
    square = (tile_cols, tile_cols)
    same = lax.broadcasted_iota(jnp.int32, square, 0) == lax.broadcasted_iota(jnp.int32, square, 1)
    real_key = jnp.max(jnp.where(same, mask[...], 0), axis=1, keepdims=True) > 0
    lane = lax.broadcasted_iota(jnp.int32, (tile_cols, lanes), 1)
    kept = real_key & (lane >= bins) & (lane < bins + heads)

    def attend(t, carry):
        some = pl.ds(pl.multiple_of(t * group, group), group)
        rows = pl.ds(pl.multiple_of(t * group * tile_cols, group * tile_cols), group * tile_cols)
        product = queries[some][:, None, :] * keys[...][None]
        product = product.reshape(group * tile_cols, width).astype(BF16)
        scores = (dot(product, gather[...]) + own[rows]).reshape(group, tile_cols, lanes)
        scores = jnp.where(kept[None], scores, -1000000000.0)
        top = jnp.max(scores, axis=1)
        raised = jnp.exp(scores - top[:, None, :])
        total = jnp.sum(raised, axis=1)
        wide = dot(raised.reshape(group * tile_cols, lanes).astype(BF16), spread[...])
        summed = jnp.sum(wide.reshape(group, tile_cols, width) * vals[...][None], axis=1)
        lane = lax.broadcasted_iota(jnp.int32, (group, lanes), 1)
        parts[c, some, 0:lanes] = jnp.where(lane < bins, pltpu.roll(total, lanes - bins, 1), top)
        parts[c, some, lanes:] = summed
        return carry

    lax.fori_loop(0, tile_rows // group, attend, 0)

    def part_copy(source, target):
        return pltpu.make_async_remote_copy(
            src_ref=parts.at[source], dst_ref=parts.at[source],
            send_sem=part_send.at[target], recv_sem=part_recv.at[source],
            device_id=(g, r, target), device_id_type=MESH,
        )

    for step in range(1, side):
        part_copy(c, lax.rem(c + step, side)).start()

    lane = lax.broadcasted_iota(jnp.int32, (tile_rows, lanes), 1)
    lower_lanes = lane < bins
    same_half = (lax.broadcasted_iota(jnp.int32, (lanes, lanes), 0) < bins) == (
        lax.broadcasted_iota(jnp.int32, (lanes, lanes), 1) < bins
    )
    adder = jnp.where(same_half, 1.0, 0.0).astype(BF16)

    def finish(u, carry):
        @pl.when(off)
        def _():
            direct(u).wait_recv()

        raised = []
        for s in range(block):
            j = u * block + s
            near = own[pl.ds(j, tile_rows, stride=tile_cols), :]
            far = own[pl.ds(j + tile_cols // 2, tile_rows, stride=tile_cols), :]
            coded = mirrored[pl.ds(pl.multiple_of(j * tile_rows, tile_rows), tile_rows)].astype(F32)
            size = jnp.exp2(jnp.log(jnp.abs(coded)) * (0.2 / math.log(2.0)) + 2.0)
            other = jnp.where(coded < 0, -size, size)
            logits = jnp.where(lower_lanes, near, pltpu.roll(far, bins, 1)) + other
            top = jnp.where(
                lower_lanes,
                jnp.max(jnp.where(lower_lanes, logits, -jnp.inf), axis=-1, keepdims=True),
                jnp.max(jnp.where(lower_lanes, -jnp.inf, logits), axis=-1, keepdims=True),
            )
            raised.append(jnp.exp(logits - top))
        value = jnp.concatenate(raised, axis=0)
        value = value / dot(value.astype(BF16), adder)
        for s in range(block):
            result[pl.ds(u * block + s, tile_rows, stride=tile_cols // 2), :] = value[
                s * tile_rows : (s + 1) * tile_rows
            ]
        return carry

    lax.fori_loop(0, chunks, finish, 0)

    for step in range(1, side):
        part_copy(lax.rem(c + step, side), lax.rem(c + step, side)).wait_recv()
    top = parts[0, :, 0:lanes]
    for k in range(1, side):
        top = jnp.maximum(top, parts[k, :, 0:lanes])
    factors = []
    total = jnp.zeros((tile_rows, lanes), F32)
    for k in range(side):
        stats = parts[k, :, 0:lanes]
        factor = jnp.exp(stats - top)
        total = total + factor * pltpu.roll(stats, bins, 1)
        factors.append(factor)
    real = (lane >= bins) & (lane < bins + heads)
    inverse = 1.0 / jnp.where(real, total, 1.0)
    attended = jnp.zeros((tile_rows, width), F32)
    for k in range(side):
        high, low = split(jnp.where(real, factors[k] * inverse, 0.0))
        attended = attended + (dot(high, spread[...]) + dot(low, spread[...])) * parts[k, :, lanes:]
    gated_out[...] = (jax.nn.sigmoid(gates[...]) * attended).astype(BF16)

    for step in range(1, side):
        part_copy(c, lax.rem(c + step, side)).wait_send()

    @pl.when(off)
    def _():
        for q in range(chunks):
            direct(q).wait_send()

    @pl.when(diagonal)
    def _():
        for t in range(len(relayed)):
            for step in range(1, side):
                forward(lax.rem(r + step, side), t).wait_send()


def unpack(packed, gated, attention_out, dist, update):
    count, tile_cols, bins = dist.shape
    value = packed[...].reshape(count, tile_cols // 2, 2 * bins)
    dist[:, : tile_cols // 2] = value[:, :, :bins]
    dist[:, tile_cols // 2 :] = value[:, :, bins:]

    @pl.when(pl.program_id(0) == 0)
    def _():
        update[...] = dot(gated[...], attention_out[...]).astype(BF16)


def body(
    side, pair, single, token_mask, pair_gain, transition_in, transition_out, bias_weight,
    bin_weight, single_gain, attention_in, attention_out,
):
    tile_rows, tile_cols, channels = pair.shape
    width = single.shape[1]
    bins = bin_weight.shape[1]
    rows = tile_rows * tile_cols
    chunks = 8
    relayed = (0, 2, 4, 6)
    n = rows // 2 // chunks
    hidden = transition_out.shape[0]
    whole = pl.BlockSpec(memory_space=pltpu.VMEM)
    dma = pltpu.SemaphoreType.DMA
    operands = (
        pair.reshape(rows, channels), single, token_mask.reshape(1, tile_cols),
        pair_gain.reshape(1, -1), transition_in, transition_out, bias_weight.T, bin_weight.T,
        single_gain, attention_in,
    )
    probabilities, gated = pl.pallas_call(
        functools.partial(kernel, side, chunks, relayed),
        out_shape=(
            jax.ShapeDtypeStruct((rows // 2, channels), F32),
            jax.ShapeDtypeStruct((tile_rows, width), BF16),
        ),
        in_specs=[pl.BlockSpec(memory_space=pltpu.HBM)] * 10,
        out_specs=(whole, whole),
        scratch_shapes=[
            *[pltpu.VMEM(operand.shape, operand.dtype) for operand in operands],
            dma((2, chunks)), dma((len(operands) - 1,)),
            pltpu.VMEM((rows, channels), F32),
            pltpu.VMEM((rows // 2, channels), BF16),
            pltpu.VMEM((rows // 2, channels), BF16),
            pltpu.VMEM((side, len(relayed) * n, channels), BF16),
            pltpu.VMEM((tile_cols, width), BF16),
            pltpu.VMEM((side, tile_rows, channels + width), F32),
            pltpu.VMEM((channels, 2 * hidden), BF16),
            pltpu.VMEM((hidden + channels, 2 * channels), BF16),
            pltpu.VMEM((4 * n, channels), BF16),
            pltpu.VMEM((4 * n, hidden), BF16),
            pltpu.VMEM((tile_rows, width), F32),
            pltpu.VMEM((tile_rows, width), F32),
            pltpu.VMEM((tile_cols, width), F32),
            pltpu.VMEM((tile_cols, width), F32),
            pltpu.VMEM((channels, width), BF16),
            pltpu.VMEM((width, channels), BF16),
            dma, dma, dma((chunks,)), dma((chunks,)),
            dma((side, len(relayed))), dma((side, len(relayed))), dma((side,)), dma((side,)),
        ],
        compiler_params=pltpu.CompilerParams(
            collective_id=0, has_side_effects=True, vmem_limit_bytes=57 << 20
        ),
    )(*operands)
    steps = 2
    some = tile_rows // steps
    return pl.pallas_call(
        unpack,
        grid=(steps,),
        out_shape=(
            jax.ShapeDtypeStruct((tile_rows, tile_cols, bins), F32),
            jax.ShapeDtypeStruct((tile_rows, width), BF16),
        ),
        in_specs=[
            pl.BlockSpec((some * tile_cols // 2, channels), lambda i: (i, 0)),
            pl.BlockSpec((tile_rows, width), lambda i: (0, 0)),
            pl.BlockSpec((width, width), lambda i: (0, 0)),
        ],
        out_specs=(
            pl.BlockSpec((some, tile_cols, bins), lambda i: (i, 0, 0)),
            pl.BlockSpec((tile_rows, width), lambda i: (0, 0)),
        ),
        compiler_params=pltpu.CompilerParams(vmem_limit_bytes=57 << 20),
    )(probabilities, gated, attention_out)


def solution(mesh):
    in_specs = (
        P(("groups", "row"), "col", None),
        P(("groups", "row"), None),
        P(("groups", "col")),
        P(), P(), P(), P(), P(), P(), P(), P(),
    )
    out_specs = (P(("groups", "row"), "col", None), P(("groups", "row"), None))
    return jax.shard_map(
        functools.partial(body, mesh.shape["row"]),
        mesh=mesh, in_specs=in_specs, out_specs=out_specs, check_vma=False,
    )
```
